256 devices in a mesh: dp: 2 (over z_lo), seq: 32 (over y, x, core), head: 4 (over z_hi).
Axes of the slice: x: 4, y: 4, z: 8 (z_hi: 4, z_lo: 2; z = z_hi * 2 + z_lo), core: 2. Of those that a mesh axis runs over, the one named last changes fastest.
Arguments:
- query_rows: bfloat16 [2, 8192, 4096], P('dp', 'seq', 'head'), may hold values from -0.59765625 to 0.59765625
- key_rows: bfloat16 [2, 8192, 4096], P('dp', 'seq', 'head'), may hold values from -0.59765625 to 0.59765625
- value_rows: bfloat16 [2, 8192, 4096], P('dp', 'seq', 'head'), may hold values from -1536 to 1536
- grad_out: bfloat16 [2, 8192, 6144], P('dp', 'seq'), may hold values from -6 to 6
- out_weight: bfloat16 [6144, 4096], P('seq', 'head'), may hold values from -0.09375 to 0.09375
- decay_rates: float32 [32], P('head'), may hold values from 0 to 1, as said below
- doc_blocks: int32 [2, 64], P('dp'), may hold values from 0 to 7, never falling along the last dimension, each value on 1 to 32 neighbouring positions
Outputs:
- grad_query: bfloat16 [2, 8192, 4096], P('dp', 'seq', 'head')
- grad_key: bfloat16 [2, 8192, 4096], P('dp', 'seq', 'head')
- grad_value: bfloat16 [2, 8192, 4096], P('dp', 'seq', 'head')
- grad_weight: float32 [6144, 4096], P('seq', 'head')
The draws below stay inside these ranges and needn't reach their ends.
Inputs may be any that keep to these rules, and one draw needn't show every extreme that they name: `doc_blocks`: in each pack document numbers never fall from block to block; every document covers 1 to 32 blocks, and one covers exactly 32. `decay_rates`: rates are positive.
All inputs are finite; a program needn't handle non-finite values.
Results may differ from the reference program's by a relative error of at most 0.024.
Values may be sent and summed in bfloat16 or wider, within the bound.
No kernel may reach another device: no remote copies, remote signals or barrier semaphores. Data moves between devices by JAX's collectives and lax.ppermute only.
A program may use at most 192 MiB of HBM per device.

```python
import math
import jax
import jax.numpy as jnp
import numpy as np
from jax import lax

D = 6144
DH = 128
HEADS = 32
BLOCK = 128
TOK_DEV = 256
PACKS = 2
SEQ_LEN = 8192
BLOCKS = 64
N_SEQ = 32


BIG_LEVEL = 256.0


def draw_decay_rates(key, part):
    slow_key, fast_key, pick_key = jax.random.split(jax.random.fold_in(key, 17), 3)
    length = float(SEQ_LEN)
    span = float(TOK_DEV)
    slow = jnp.exp(jax.random.uniform(slow_key, (HEADS,), jnp.float32, math.log(0.3 / length), math.log(2.0 / length)))
    fast = jnp.exp(jax.random.uniform(fast_key, (HEADS,), jnp.float32, math.log(3.0), math.log(7.0))) / span
    share = 0.5
    chosen = jax.random.uniform(pick_key, (HEADS,), jnp.float32) < share
    return jnp.where(chosen, slow, fast).astype(jnp.float32)


def draw_value_rows(key, part):
    base_key, phase_key = jax.random.split(jax.random.fold_in(key, 29))
    shape = (PACKS, SEQ_LEN, HEADS * DH)
    base = jnp.clip(jax.random.normal(base_key, shape, jnp.float32), -6.0, 6.0)
    phase = jax.random.randint(phase_key, (PACKS, 1), 0, 3).astype(jnp.int32)
    span_number = (jnp.arange(SEQ_LEN).astype(jnp.int32) // TOK_DEV)[None, :]
    level = jnp.where((span_number + phase) % 3 == 0, BIG_LEVEL, 1.0).astype(jnp.float32)
    return (base * level[:, :, None]).astype(jnp.bfloat16)


def spiked(entries, key, source, target, shards_of, factor):
    owner, partner = [(jnp.arange(entries.shape[dim]) // (entries.shape[dim] // shards_of)).reshape([-1 if axis == dim else 1 for axis in range(entries.ndim)]) for dim in (source, target)]
    chosen = jax.random.permutation(key, shards_of)[partner]
    strong = (owner == chosen) | (owner == (partner + shards_of // 2) % shards_of)
    return jnp.where(strong, factor * entries, entries)


def block_scale(own_key, extent, cuts, least, top_value):
    factor_of = 1.0
    for dim, parts in cuts:
        steps = jax.random.uniform(jax.random.fold_in(jax.random.fold_in(own_key, 6), dim), (parts,), jnp.float32, least / len(cuts), top_value / len(cuts))
        factor_of = factor_of * jnp.repeat(jnp.exp(steps), extent[dim] // parts).reshape((-1,) + (1,) * (len(extent) - 1 - dim))
    return factor_of


def length_profile(count, total, reach, lean):
    portions = [(1 << 20) // math.isqrt(grade ** lean) + 1 for grade in range(2, count + 1)]
    rest, given = total - reach - (count - 1), [1] * (count - 1)
    while rest > 0:
        candidates = [i for i in range(count - 1) if given[i] < reach]
        pool, left = sum([portions[i] for i in candidates]), rest
        for i in candidates:
            extra = min(reach - given[i], max(1, left * portions[i] // pool), rest)
            given[i] = given[i] + extra
            rest = rest - extra
    return np.array([reach] + given)


def ragged(key, amount, total, most, slope):
    if amount == 2:
        one = jax.random.randint(key, (), max(1, total - most), min(most, total - 1) + 1)
        return jnp.stack([one, total - one])
    sizes = jnp.asarray(length_profile(amount, total, most, slope), jnp.int32)
    pairs = (amount - 1) // 2
    giver, taker = sizes[1:1 + 2 * pairs:2], sizes[2:2 + 2 * pairs:2]
    room = jnp.minimum(giver - 1, most - taker)
    moved = jax.random.randint(jax.random.fold_in(key, 1), (pairs,), 0, 1 << 20) % (room + 1)
    sizes = sizes.at[1:1 + 2 * pairs:2].set(giver - moved).at[2:2 + 2 * pairs:2].set(taker + moved)
    return sizes[jax.random.permutation(jax.random.fold_in(key, 2), amount)]


def noise(own_key, extent, width, limit, cuts=(), dtype=jnp.bfloat16):
    values = width * jax.random.normal(own_key, extent, jnp.float32)
    if cuts:
        values = values * block_scale(own_key, extent, cuts, -0.22, 0.18)
    return jnp.clip(values, -limit, limit).astype(dtype)


def gaussian_with(key, dims, width, limit, shards, heavy, dtype=jnp.bfloat16):
    values = width * jax.random.normal(key, dims, jnp.float32)
    if shards:
        values = values * block_scale(key, dims, shards, -0.22, 0.18)
    return jnp.clip(spiked(values, jax.random.fold_in(key, 3), *heavy), -limit, limit).astype(dtype)


def setup_inputs(seed: int = 0) -> dict:
    splits = jax.random.split(jax.random.key(seed), 8)
    return {
        "query_rows": noise(splits[0], (PACKS, SEQ_LEN, HEADS * DH), 0.09, 0.59765625, ((0, 2), (1, 32), (2, 4))),
        "key_rows": noise(splits[1], (PACKS, SEQ_LEN, HEADS * DH), 0.09, 0.59765625, ((0, 2), (1, 32), (2, 4))),
        "value_rows": draw_value_rows(jax.random.fold_in(splits[7], 71), 0),
        "grad_out": gaussian_with(splits[3], (PACKS, SEQ_LEN, D), 1.0, 6.0, ((0, 2), (1, 32)), (1, 2, 32, 2.75)),
        "out_weight": noise(splits[4], (D, HEADS * DH), (HEADS * DH) ** -0.5, 0.09375, ((0, 32), (1, 4))),
        "decay_rates": draw_decay_rates(jax.random.fold_in(splits[7], 71), 0),
        "doc_blocks": jax.vmap(lambda own: jnp.searchsorted(jnp.cumsum(ragged(own, max(2, N_SEQ // 4), BLOCKS, BLOCKS // 2, 2)), jnp.arange(BLOCKS), side="right"))(jax.random.split(splits[6], PACKS)).reshape((PACKS, BLOCKS)).astype(jnp.int32),
    }


EPSILON = 1e-05

def rounded(array):
    return lax.optimization_barrier(array.astype(jnp.bfloat16))

def block_docs(doc_row, first_block, block_count, block_len):
    blocks = lax.dynamic_slice_in_dim(doc_row, first_block, block_count)
    return jnp.reshape(jnp.broadcast_to(blocks[:, None], (block_count, block_len)), (block_count * block_len,))

def decay_masks(token_docs, decay_rates, prev_doc, next_doc):
    length = token_docs.shape[0]
    position = jnp.arange(length).astype(jnp.float32)
    rates = decay_rates.astype(jnp.float32)[:, None]
    distance = position[:, None] - position[None, :]
    allowed = jnp.logical_and(distance >= 0, token_docs[:, None] == token_docs[None, :])
    intra = jnp.where(allowed[None], jnp.exp(-rates[:, :, None] * jnp.maximum(distance, 0.0)[None]), 0.0)
    weight_end = jnp.where((token_docs == token_docs[length - 1])[None], jnp.exp(-rates * (length - 1.0 - position)[None]), 0.0)
    weight_start = jnp.where((token_docs == token_docs[0])[None], jnp.exp(-rates * position[None]), 0.0)
    weight_before = jnp.where((token_docs == prev_doc)[None], jnp.exp(-rates * (position + 1.0)[None]), 0.0)
    weight_after = jnp.where((token_docs == next_doc)[None], jnp.exp(-rates * (length - position)[None]), 0.0)
    span_decay = jnp.exp(-decay_rates.astype(jnp.float32) * float(length))
    link_fwd = jnp.where(token_docs[length - 1] == prev_doc, span_decay, 0.0)
    link_rev = jnp.where(token_docs[0] == next_doc, span_decay, 0.0)
    return (intra, weight_end, weight_start, weight_before, weight_after, link_fwd, link_rev)

def local_state(keys_here, values_here, weight_end):
    weighted = rounded(keys_here.astype(jnp.float32) * weight_end.T[:, :, None])
    return jnp.einsum('jhd,jhe->hde', weighted.astype(jnp.float32), values_here.astype(jnp.float32))

def forward_out(queries, keys_here, values_here, intra, weight_before, state_in):
    scores = jnp.einsum('thd,jhd->htj', queries.astype(jnp.float32), keys_here.astype(jnp.float32))
    attention = rounded(scores * intra)
    state_low = rounded(state_in)
    carried = jnp.einsum('thd,hde->the', queries.astype(jnp.float32), state_low.astype(jnp.float32))
    output = jnp.einsum('htj,jhe->the', attention.astype(jnp.float32), values_here.astype(jnp.float32)) + weight_before.T[:, :, None] * carried
    inverse_rms = lax.rsqrt(lax.optimization_barrier(jnp.mean(output * output, axis=-1, keepdims=True)) + EPSILON)
    return (attention, state_low, output * inverse_rms, inverse_rms)

def backward_local(queries, values_here, intra, normal, inverse_rms, grad_normed, weight_start):
    inner = lax.optimization_barrier(jnp.mean(grad_normed * normal, axis=-1, keepdims=True))
    grad_attn = rounded(inverse_rms * (grad_normed - normal * inner))
    grad_scores = rounded(jnp.einsum('the,jhe->htj', grad_attn.astype(jnp.float32), values_here.astype(jnp.float32)) * intra)
    weighted = rounded(queries.astype(jnp.float32) * weight_start.T[:, :, None])
    back_local = jnp.einsum('thd,the->hde', weighted.astype(jnp.float32), grad_attn.astype(jnp.float32))
    return (grad_attn, grad_scores, back_local)

def backward_rest(queries, keys_here, values_here, attention, state_low, grad_attn, grad_scores, weight_before, weight_after, state_back):
    back_low = rounded(state_back).astype(jnp.float32)
    attn_f = grad_attn.astype(jnp.float32)
    score_f = grad_scores.astype(jnp.float32)
    grad_query = jnp.einsum('htj,jhd->thd', score_f, keys_here.astype(jnp.float32)) + weight_before.T[:, :, None] * jnp.einsum('the,hde->thd', attn_f, state_low.astype(jnp.float32))
    grad_key = jnp.einsum('htj,thd->jhd', score_f, queries.astype(jnp.float32)) + weight_after.T[:, :, None] * jnp.einsum('jhe,hde->jhd', values_here.astype(jnp.float32), back_low)
    grad_value = jnp.einsum('htj,the->jhe', attention.astype(jnp.float32), attn_f) + weight_after.T[:, :, None] * jnp.einsum('jhd,hde->jhe', keys_here.astype(jnp.float32), back_low)
    return (grad_query.astype(jnp.bfloat16), grad_key.astype(jnp.bfloat16), grad_value.astype(jnp.bfloat16))

def reference(query_rows, key_rows, value_rows, grad_out, out_weight, decay_rates, doc_blocks):
    block_count = TOK_DEV // BLOCK
    norm_factor = (PACKS * SEQ_LEN) ** (-0.5)
    weight_sum = jnp.zeros((D, HEADS * DH), jnp.float32)
    query_list, key_list, value_list = ([], [], [])
    span_ids = jnp.arange(N_SEQ).astype(jnp.int32)
    for pack_index in range(PACKS):
        queries = query_rows[pack_index].reshape(N_SEQ, TOK_DEV, HEADS, DH)
        keys_all = key_rows[pack_index].reshape(N_SEQ, TOK_DEV, HEADS, DH)
        values_all = value_rows[pack_index].reshape(N_SEQ, TOK_DEV, HEADS, DH)
        doc_row = doc_blocks[pack_index]

        def span_masks(span_index, doc_row=doc_row):
            first_block = (span_index * block_count).astype(jnp.int32)
            token_docs = block_docs(doc_row, first_block, block_count, BLOCK)
            prev_doc = doc_row[jnp.maximum(first_block - 1, 0)]
            next_doc = doc_row[jnp.minimum(first_block + block_count, BLOCKS - 1)]
            return decay_masks(token_docs, decay_rates, prev_doc, next_doc)

        def forward_step(state_in, inputs, span_masks=span_masks):
            span_index, query_span, key_span, value_span = inputs
            mask_set = span_masks(span_index)
            state_local = local_state(key_span, value_span, mask_set[1])
            attention, state_low, normal, inverse_rms = forward_out(query_span, key_span, value_span, mask_set[0], mask_set[3], state_in)
            state_out = mask_set[5][:, None, None] * state_in + state_local
            return (state_out, (state_in, normal.astype(jnp.bfloat16)))
        start_state = jnp.zeros((HEADS, DH, DH), jnp.float32)
        final_state, (states_in, normed) = lax.scan(forward_step, start_state, (span_ids, queries, keys_all, values_all))
        normed_flat = normed.reshape(N_SEQ, TOK_DEV, HEADS * DH)
        grads_pack = grad_out[pack_index].reshape(N_SEQ, TOK_DEV, D)

        def weight_step(running, inputs):
            grad_span, normed_span = inputs
            part = rounded(jnp.dot(grad_span.T, normed_span, preferred_element_type=jnp.float32)).astype(jnp.float32)
            return (running + part, 0)
        weight_sum, ignored = lax.scan(weight_step, weight_sum, (grads_pack, normed_flat))
        grad_normed_all = jnp.dot(grad_out[pack_index], out_weight, preferred_element_type=jnp.float32).reshape(N_SEQ, TOK_DEV, HEADS, DH)

        def backward_step(state_back, inputs, span_masks=span_masks):
            span_index, query_span, key_span, value_span, state_in, grad_normed = inputs
            mask_set = span_masks(span_index)
            attention, state_low, normal, inverse_rms = forward_out(query_span, key_span, value_span, mask_set[0], mask_set[3], state_in)
            grad_attn, grad_scores, back_local = backward_local(query_span, value_span, mask_set[0], normal, inverse_rms, grad_normed, mask_set[2])
            grads = backward_rest(query_span, key_span, value_span, attention, state_low, grad_attn, grad_scores, mask_set[3], mask_set[4], state_back)
            state_next = mask_set[6][:, None, None] * state_back + back_local
            return (state_next, grads)
        final_back, (grad_query, grad_key, grad_value) = lax.scan(backward_step, start_state, (span_ids, queries, keys_all, values_all, states_in, grad_normed_all), reverse=True)
        query_list.append(grad_query.reshape(SEQ_LEN, HEADS * DH))
        key_list.append(grad_key.reshape(SEQ_LEN, HEADS * DH))
        value_list.append(grad_value.reshape(SEQ_LEN, HEADS * DH))
    return (jnp.stack(query_list), jnp.stack(key_list), jnp.stack(value_list), weight_sum * norm_factor)
```

```python
import jax
import jax.numpy as jnp
from jax import lax
from jax.experimental import pallas as pl
from jax.experimental.pallas import tpu as pltpu
from jax.sharding import PartitionSpec as P

EPSILON = 1e-05
TOK = 256
HEADS = 8
DH = 128
FEAT = HEADS * DH
HALF = FEAT // 2
ROWS = 192
CHIPS = 16
REL = (0, 3, 1, 2)
BF = jnp.bfloat16
F32 = jnp.float32


def ring(move):
    pairs = []
    for y in range(4):
        for x in range(4):
            for c in range(2):
                ty, tx, tc = move(y, x, c)
                pairs.append((((y * 4) + x) * 2 + c, ((ty % 4) * 4 + tx % 4) * 2 + tc))
    return pairs


PARTNER = ring(lambda y, x, c: (y, x, 1 - c))


def x_by(n):
    return ring(lambda y, x, c: (y, x + n, c))


def y_by(n):
    return ring(lambda y, x, c: (y + n, x, c))


def first_by(n):
    return ring(lambda y, x, c: (y, x + n, c) if c == 0 else (y + n, x, c))


def second_by(n):
    return ring(lambda y, x, c: (y + n, x, c) if c == 0 else (y, x + n, c))


def send(array, pairs):
    return lax.ppermute(array, "seq", pairs)


def dot(a, b, dims=((1,), (0,))):
    return lax.dot_general(a, b, (dims, ((), ())), preferred_element_type=F32)


NT = ((1,), (1,))
TN = ((0,), (0,))


def call(body, outs, operands, smem=(), flops=0, name=None):
    vmem = pl.BlockSpec(memory_space=pltpu.VMEM)
    sm = pl.BlockSpec(memory_space=pltpu.SMEM)
    nbytes = sum(a.size * a.dtype.itemsize for a in operands) + sum(
        o.size * o.dtype.itemsize for o in outs
    )
    return pl.pallas_call(
        body,
        out_shape=outs,
        in_specs=[sm] * len(smem) + [vmem] * len(operands),
        out_specs=[vmem] * len(outs),
        compiler_params=pltpu.CompilerParams(vmem_limit_bytes=48 << 20),
        cost_estimate=pl.CostEstimate(flops=flops, bytes_accessed=nbytes, transcendentals=0),
        name=name,
    )(*smem, *operands)


def shape(*dims, dtype=BF):
    return jax.ShapeDtypeStruct(dims, dtype)


def head(h):
    return slice(h * DH, (h + 1) * DH)


def position():
    return lax.broadcasted_iota(jnp.int32, (TOK, DH), 0)


def column(rate, offset, low_flag, high_flag):
    row = position()
    flag = jnp.where(row < TOK // 2, low_flag, high_flag)
    return jnp.where(flag > 0, jnp.exp(-rate * offset.astype(F32)), 0.0)


def intra_mask(same):
    t = lax.broadcasted_iota(jnp.int32, (TOK, TOK), 0)
    j = lax.broadcasted_iota(jnp.int32, (TOK, TOK), 1)
    distance = t - j
    half = TOK // 2
    crossing = jnp.logical_and(t >= half, j < half)
    allowed = jnp.logical_and(
        distance >= 0, jnp.logical_or(jnp.logical_not(crossing), same > 0)
    )
    return jnp.maximum(distance, 0).astype(F32), allowed


def where_am_i():
    span = lax.axis_index("seq")
    chip = lax.div(span, 2)
    return lax.rem(span, 2), lax.div(chip, 4), lax.rem(chip, 4)


def doc_flags(docs):
    span = lax.axis_index("seq")
    first, second = docs[2 * span], docs[2 * span + 1]
    prev = docs[jnp.maximum(2 * span - 1, 0)]
    coming = docs[jnp.minimum(2 * span + 2, 63)]
    tests = (first == second, first == prev, second == prev, first == coming, second == coming)
    return [jnp.where(t, 1, 0) for t in tests]


def lanes(h):
    return pl.ds(pl.multiple_of(h * DH, DH), DH)


def local_state_body(rates, docs, k, v, own, theirs):
    flags = doc_flags(docs)
    core, _, _ = where_am_i()
    for i in range(HEADS):
        h = lax.rem(core * 4 + i, HEADS)
        w = column(rates[h], TOK - 1 - position(), flags[0], 1)
        weighted = (k[:, lanes(h)].astype(F32) * w).astype(BF)
        state = dot(weighted, v[:, lanes(h)], TN)
        if i < 4:
            own[head(i), :] = state
        else:
            theirs[head(i - 4), :] = state.astype(BF)


def local_out_body(rates, docs, q, k, v, att, out):
    flags = doc_flags(docs)
    core, _, _ = where_am_i()
    distance, allowed = intra_mask(flags[0])
    for h in range(HEADS):
        intra = jnp.where(allowed, jnp.exp(-rates[h] * distance), 0.0)
        a = (dot(q[:, head(h)], k[:, head(h)], NT) * intra).astype(BF)
        att[h] = a
        out[:, head(h)] = dot(a, v[:, head(h)])


def pick(core, h, own, other):
    rows = slice((h % 4) * DH, (h % 4 + 1) * DH)
    mine = core == (h // 4)
    return jnp.where(mine, own[rows, :].astype(F32), other[rows, :].astype(F32)).astype(BF)


def forward_body(rates, docs, q, local, own, other, out, normed):
    flags = doc_flags(docs)
    core, _, _ = where_am_i()
    for h in range(HEADS):
        w = column(rates[h], position() + 1, flags[1], flags[2])
        o = local[:, head(h)] + w * dot(q[:, head(h)], pick(core, h, own, other))
        out[:, head(h)] = o
        inv = lax.rsqrt(jnp.mean(o * o, axis=-1, keepdims=True) + EPSILON)
        normed[:, head(h)] = (o * inv).astype(BF)


def grad_attn_body(rates, docs, q, out, part, part_other, grad, own, theirs):
    flags = doc_flags(docs)
    core, _, _ = where_am_i()
    for i in range(HEADS):
        h = lax.rem(core * 4 + i, HEADS)
        at = lanes(h)
        o = out[:, at]
        inv = lax.rsqrt(jnp.mean(o * o, axis=-1, keepdims=True) + EPSILON)
        normal = o * inv
        g = part[:, at] + part_other[:, at].astype(F32)
        inner = jnp.mean(g * normal, axis=-1, keepdims=True)
        ga = (inv * (g - normal * inner)).astype(BF)
        grad[:, at] = ga
        w = column(rates[h], position(), 1, flags[0])
        weighted = (q[:, at].astype(F32) * w).astype(BF)
        state = dot(weighted, ga, TN)
        if i < 4:
            own[head(i), :] = state
        else:
            theirs[head(i - 4), :] = state.astype(BF)


def grad_local_body(rates, docs, q, k, v, att, grad, own, other, dq, dk, dv):
    flags = doc_flags(docs)
    core, _, _ = where_am_i()
    distance, allowed = intra_mask(flags[0])
    for h in range(HEADS):
        intra = jnp.where(allowed, jnp.exp(-rates[h] * distance), 0.0)
        ga = grad[:, head(h)]
        ds = (dot(ga, v[:, head(h)], NT) * intra).astype(BF)
        w = column(rates[h], position() + 1, flags[1], flags[2])
        dq[:, head(h)] = (
            dot(ds, k[:, head(h)]) + w * dot(ga, pick(core, h, own, other), NT)
        ).astype(BF)
        dk[:, head(h)] = dot(ds, q[:, head(h)], TN)
        dv[:, head(h)] = dot(att[h], ga, TN)


def grad_rest_body(rates, docs, k, v, dkl, dvl, own, other, dk, dv):
    flags = doc_flags(docs)
    core, _, _ = where_am_i()
    for h in range(HEADS):
        w = column(rates[h], TOK - position(), flags[3], flags[4])
        back = pick(core, h, own, other)
        dk[:, head(h)] = (dkl[:, head(h)] + w * dot(v[:, head(h)], back, NT)).astype(BF)
        dv[:, head(h)] = (dvl[:, head(h)] + w * dot(k[:, head(h)], back)).astype(BF)


def split_body(g, mine, theirs, mine_t, theirs_t, gm, gmt, gt):
    core, y, x = where_am_i()
    first, second = jnp.where(core == 0, x, y), jnp.where(core == 0, y, x)
    step, stride = jnp.where(core == 0, 1, 4), jnp.where(core == 0, 4, 1)

    def pair(p, first, second, step, stride):
        at = lax.rem(second + REL[p // 2], 4) * stride
        cols = []
        for k in (2 * (p % 2), 2 * (p % 2) + 1):
            chip = at + lax.rem(first + REL[k], 4) * step
            cols.append(g[:, pl.ds(pl.multiple_of(chip * 2 * ROWS, DH), 2 * ROWS)])
        return jnp.concatenate(cols, 1)

    for p in range(8):
        block = pair(p, first, second, step, stride)
        gm[p] = dot(block, mine[...]).astype(BF)
        gmt[p] = dot(mine_t[...], block, NT).astype(BF)
        block = pair(p, second, first, stride, step)
        gt[p, :TOK, :] = dot(block, theirs[...]).astype(BF)
        gt[p, TOK:, :TOK] = dot(theirs_t[...], block, NT).astype(BF)


def join_body(*refs):
    out, at = refs[-1], 0
    for ref in refs[:-1]:
        out[at : at + ref.shape[0], :] = ref[...]
        at += ref.shape[0]


def join(*arrays):
    rows = sum(a.shape[0] for a in arrays)
    return call(join_body, [shape(rows, arrays[0].shape[1])], arrays, name="join")[0]


def project_body(received, out_dtype):
    def body(g, *refs):
        weights, out = refs[:8], refs[8]
        total = None
        for p in range(8):
            d = dot(g[p, :TOK, :] if received else g[p], weights[p][...])
            total = d if total is None else total + d
        out[...] = total.astype(out_dtype)

    return body


def part_of(gm, gr, nm, nr, p):
    return dot(gm[p], nm[...]) + dot(gr[p, TOK:, :TOK], nr[...])


def scatter_two_body(p, q):
    def body(gm, gr, nm, nr, a, b):
        a[...] = part_of(gm, gr, nm, nr, p).astype(BF)
        b[...] = part_of(gm, gr, nm, nr, q).astype(BF)

    return body


def scatter_near_body(gm, gr, nm, nr, from_minus, from_plus, plus, minus):
    plus[...] = (part_of(gm, gr, nm, nr, 4) + from_minus[...].astype(F32)).astype(BF)
    minus[...] = (part_of(gm, gr, nm, nr, 3) + from_plus[...].astype(F32)).astype(BF)


def scatter_own_body(gm, gr, nm, nr, low0, low1, high0, high1, mine, minus, plus, far0, far1):
    v = part_of(gm, gr, nm, nr, 0) + low0[...].astype(F32) + low1[...].astype(F32)
    mine[...] = v[:ROWS]
    minus[...] = v[ROWS:].astype(BF)
    v = part_of(gm, gr, nm, nr, 1) + high0[...].astype(F32) + high1[...].astype(F32)
    plus[...] = v[:ROWS].astype(BF)
    cut = ROWS + ROWS // 2
    far0[...] = v[ROWS:cut].astype(BF)
    far1[...] = v[cut:].astype(BF)


def last_plus_body(plus, minus, from_minus, from_plus, plus_out, minus_out):
    cut = ROWS // 2
    plus_out[:cut, :] = plus[:cut, :] + from_minus[...]
    plus_out[cut:, :] = plus[cut:, :]
    minus_out[:cut, :] = minus[:cut, :]
    minus_out[cut:, :] = minus[cut:, :] + from_plus[...]


def last_sum_body(own, from_minus, from_plus, out):
    out[...] = (own[...] + from_minus[...].astype(F32) + from_plus[...].astype(F32)).astype(BF)


def scan_tools(rates, docs, backward):
    core, y, x = where_am_i()
    half = core * 4
    if backward:
        core, y, x = 1 - core, 3 - y, 3 - x

    def doc(s):
        s = jnp.clip(s, 0, 31)
        return docs[62 - 2 * s] if backward else docs[2 * s + 1]

    def weight(h, steps, one, two, valid=True):
        equal = jnp.logical_and(doc(one) == doc(two), valid)
        steps = jnp.maximum(steps, 0).astype(F32) * float(TOK)
        decay = jnp.exp(-(rates[half + h] * steps) * jnp.ones((1, DH), F32))
        return jnp.where(equal, decay, 0.0)

    return core, y, x, y * 4 + x, weight


def scan_total_body(backward):
    def body(rates, docs, own, got, total, low):
        core, y, x, chip, weight = scan_tools(rates, docs, backward)
        for h in range(4):
            w = weight(h, jnp.int32(1), 2 * chip, 2 * chip + 1)
            first = jnp.where(core == 0, w, 1.0)
            second = jnp.where(core == 0, 1.0, w)
            t = first * own[head(h), :] + second * got[head(h), :].astype(F32)
            total[head(h), :] = t
            low[head(h), :] = t.astype(BF)

    return body


def scan_row_body(backward):
    def body(rates, docs, total, near1, near2, near3, before, low):
        core, y, x, chip, weight = scan_tools(rates, docs, backward)
        row, last, entry = y * 4, y * 8 + 7, 2 * chip - 1
        for h in range(4):
            t = total[head(h), :]
            whole = weight(h, 2 * (3 - x), 2 * chip + 1, last) * t
            ahead = jnp.zeros_like(t)
            for n, near in ((1, near1), (2, near2), (3, near3)):
                at = lax.rem(x + 4 - n, 4)
                v = near[head(h), :].astype(F32)
                whole = whole + weight(h, 2 * (3 - at), 2 * (row + at) + 1, last) * v
                ahead = ahead + weight(h, 2 * (x - 1 - at), 2 * (row + at) + 1, entry, at < x) * v
            before[head(h), :] = ahead
            low[head(h), :] = whole.astype(BF)

    return body


def scan_end_body(backward):
    def body(rates, docs, before, own, got, up1, up2, mine, other):
        core, y, x, chip, weight = scan_tools(rates, docs, backward)
        entry = 2 * chip - 1
        for h in range(4):
            ahead = before[head(h), :]
            for n, up in ((1, up1), (2, up2)):
                at = y * 4 - 4 * n + 3
                w = weight(h, 2 * (chip - 1 - at), 2 * at + 1, entry, y >= n)
                ahead = ahead + w * up[head(h), :].astype(F32)
            first = jnp.where(core == 0, own[head(h), :], got[head(h), :].astype(F32))
            after = first + weight(h, jnp.int32(1), 2 * chip, entry, chip > 0) * ahead
            mine[head(h), :] = jnp.where(core == 0, ahead, after).astype(BF)
            other[head(h), :] = jnp.where(core == 0, after, ahead).astype(BF)

    return body


WIDE, NARROW = shape(HALF, DH, dtype=F32), shape(HALF, DH)


class Scan:
    def __init__(self, sm, backward):
        self.sm, self.backward = sm, backward
        self.sign = -1 if backward else 1
        self.name = "back" if backward else "fwd"

    def total(self, own, theirs):
        self.own, self.got = own, send(theirs, PARTNER)
        self.sum, low = call(
            scan_total_body(self.backward),
            [WIDE, NARROW],
            [self.own, self.got],
            self.sm,
            name=self.name + "_total",
        )
        return low

    def along_x(self, low):
        return [send(low, x_by(self.sign * n)) for n in (1, 2, 3)]

    def row(self, near):
        self.before, low = call(
            scan_row_body(self.backward),
            [WIDE, NARROW],
            [self.sum, *near],
            self.sm,
            name=self.name + "_row",
        )
        return low

    def along_y(self, low):
        return [send(low, y_by(self.sign * n)) for n in (1, 2)]

    def end(self, up):
        mine, other = call(
            scan_end_body(self.backward),
            [NARROW, NARROW],
            [self.before, self.own, self.got, *up],
            self.sm,
            name=self.name + "_end",
        )
        return mine, send(other, PARTNER)


def after(arrays):
    return lax.optimization_barrier(tuple(arrays))


def local(query_rows, key_rows, value_rows, grad_out, out_weight, decay_rates, doc_blocks):
    q, k, v, g = query_rows[0], key_rows[0], value_rows[0], grad_out[0]
    core = lax.axis_index("seq") % 2
    sm = (decay_rates, doc_blocks[0])
    unit = 2 * HEADS * TOK * DH * DH
    states = [shape(HALF, DH, dtype=F32), shape(HALF, DH)]

    minus, plus = send(out_weight, first_by(1)), send(out_weight, first_by(-1))
    fwd = Scan(sm, False)
    low = fwd.total(*call(local_state_body, states, [k, v], sm, flops=unit, name="state_local"))
    half = ROWS // 2
    low, g, minus, plus = after((low, g, minus, plus))
    near = fwd.along_x(low)
    far_low = send(minus[:half], first_by(1))
    far_high = send(plus[half:], first_by(-1))

    r = lax.broadcasted_iota(jnp.int32, (4 * ROWS, 2 * ROWS), 0)
    c = lax.broadcasted_iota(jnp.int32, (4 * ROWS, 2 * ROWS), 1)
    source = c + jnp.where(c < ROWS, 0, ROWS)
    select = [(r == source + side * ROWS).astype(BF) for side in (core, 1 - core)]
    gm, gmt, gt = call(
        split_body,
        [shape(8, TOK, 2 * ROWS), shape(8, 2 * ROWS, TOK), shape(8, TOK + 2 * ROWS, 2 * ROWS)],
        [g, *select, *(m.T for m in select)],
        flops=16 * TOK * 6144 * ROWS,
        name="split",
    )
    *near, gm, gt, far_low, far_high = after((*near, gm, gt, far_low, far_high))
    low = fwd.row(near)
    gr = send(gt, PARTNER)
    up = fwd.along_y(low)

    own_low, own_high = join(out_weight, minus), join(plus, far_low, far_high)
    minus_low, plus_high = send(own_low, second_by(1)), send(own_high, second_by(-1))

    att, out_local = call(
        local_out_body,
        [shape(HEADS, TOK, TOK), shape(TOK, FEAT, dtype=F32)],
        [q, k, v],
        sm,
        flops=4 * unit,
        name="attend",
    )
    *up, own_low, own_high, att, out_local = after((*up, own_low, own_high, att, out_local))
    own, other = fwd.end(up)
    out, normed = call(
        forward_body,
        [shape(TOK, FEAT, dtype=F32), shape(TOK, FEAT)],
        [q, out_local, own, other],
        sm,
        flops=unit,
        name="carry",
    )
    normed_other = send(normed, PARTNER)
    own_low, own_high, minus_low, plus_high, normed_other = after(
        (own_low, own_high, minus_low, plus_high, normed_other)
    )
    minus_high, plus_low = send(own_high, second_by(1)), send(own_low, second_by(-1))

    terms = [gmt, gr, normed, normed_other]
    pair = shape(2 * ROWS, FEAT)
    chunk = 8 * TOK * ROWS * FEAT
    low, high = call(scatter_two_body(6, 7), [pair] * 2, terms, flops=2 * chunk, name="part_far")
    near_in = [send(low, second_by(1)), send(high, second_by(-1))]
    plus, minus = call(
        scatter_two_body(5, 2), [pair] * 2, terms, flops=2 * chunk, name="part_free"
    )
    minus_low, plus_high, minus_high, plus_low, plus, minus = after(
        (minus_low, plus_high, minus_high, plus_low, plus, minus)
    )
    far_low, far_high = send(minus_low, second_by(1)), send(plus_high, second_by(-1))
    weights = [own_low, own_high, minus_low, minus_high, plus_low, plus_high, far_low, far_high]
    free_in = [send(plus, second_by(1)), send(minus, second_by(-1))]
    plus, minus = call(
        scatter_near_body, [pair] * 2, terms + near_in, flops=2 * chunk, name="part_near"
    )
    late_in = [send(plus, second_by(1)), send(minus, second_by(-1))]
    project = 2 * TOK * CHIPS * ROWS * FEAT
    (theirs_part,) = call(
        project_body(True, BF), [shape(TOK, FEAT)], [gr, *weights], flops=project, name="proj_other"
    )
    part_other = send(theirs_part, PARTNER)
    (part,) = call(
        project_body(False, F32),
        [shape(TOK, FEAT, dtype=F32)],
        [gm, *weights],
        flops=project,
        name="proj_own",
    )
    grad, *back = call(
        grad_attn_body,
        [shape(TOK, FEAT), *states],
        [q, out, part, part_other],
        sm,
        flops=unit,
        name="grad_attn",
    )
    back_scan = Scan(sm, True)
    near = back_scan.along_x(back_scan.total(*back))

    terms, _ = after((tuple(terms), grad))
    block = shape(ROWS, FEAT)
    small = shape(ROWS // 2, FEAT)
    mine, minus, plus, low, high = call(
        scatter_own_body,
        [shape(ROWS, FEAT, dtype=F32), block, block, small, small],
        [*terms, late_in[0], free_in[1], free_in[0], late_in[1]],
        flops=2 * chunk,
        name="part_own",
    )
    plus, minus = call(
        last_plus_body,
        [block] * 2,
        [plus, minus, send(low, first_by(1)), send(high, first_by(-1))],
        name="part_last",
    )
    (total,) = call(
        last_sum_body,
        [block],
        [mine, send(plus, first_by(1)), send(minus, first_by(-1))],
        name="part_sum",
    )
    scale = (2 * 32 * TOK) ** (-0.5)
    swapped = lax.ppermute(total, "dp", [(0, 1), (1, 0)])
    grad_weight = (total.astype(F32) + swapped.astype(F32)) * scale

    dq, dkl, dvl = call(
        grad_local_body,
        [shape(TOK, FEAT), shape(TOK, FEAT, dtype=F32), shape(TOK, FEAT, dtype=F32)],
        [q, k, v, att, grad, own, other],
        sm,
        flops=9 * unit,
        name="grad_local",
    )
    *near, dq, dkl, dvl = after((*near, dq, dkl, dvl))
    up = back_scan.along_y(back_scan.row(near))
    back_own, back_other = back_scan.end(up)
    dk, dv = call(
        grad_rest_body,
        [shape(TOK, FEAT), shape(TOK, FEAT)],
        [k, v, dkl, dvl, back_own, back_other],
        sm,
        flops=2 * unit,
        name="grad_rest",
    )
    return dq[None], dk[None], dv[None], grad_weight


def solution(mesh):
    in_specs = (
        P("dp", "seq", "head"),
        P("dp", "seq", "head"),
        P("dp", "seq", "head"),
        P("dp", "seq", None),
        P("seq", "head"),
        P("head"),
        P("dp", None),
    )
    out_specs = (
        P("dp", "seq", "head"),
        P("dp", "seq", "head"),
        P("dp", "seq", "head"),
        P("seq", "head"),
    )
    return jax.shard_map(local, mesh=mesh, in_specs=in_specs, out_specs=out_specs, check_vma=False)
```

```python
import jax
import jax.numpy as jnp
from jax import lax
from jax.experimental import pallas as pl
from jax.experimental.pallas import tpu as pltpu
from jax.sharding import PartitionSpec as P

EPSILON = 1e-05
TOK = 256
HEADS = 8
DH = 128
FEAT = HEADS * DH
HALF = FEAT // 2
ROWS = 192
CHIPS = 16
LIMIT = 24
REL = (0, 3, 1, 2)
BF = jnp.bfloat16
F32 = jnp.float32


def ring(move):
    pairs = []
    for y in range(4):
        for x in range(4):
            for c in range(2):
                ty, tx, tc = move(y, x, c)
                pairs.append((((y * 4) + x) * 2 + c, ((ty % 4) * 4 + tx % 4) * 2 + tc))
    return pairs


PARTNER = ring(lambda y, x, c: (y, x, 1 - c))


def x_by(n):
    return ring(lambda y, x, c: (y, x + n, c))


def y_by(n):
    return ring(lambda y, x, c: (y + n, x, c))


def first_by(n):
    return ring(lambda y, x, c: (y, x + n, c) if c == 0 else (y + n, x, c))


def second_by(n):
    return ring(lambda y, x, c: (y + n, x, c) if c == 0 else (y, x + n, c))


def send(array, pairs):
    return lax.ppermute(array, "seq", pairs)


def dot(a, b, dims=((1,), (0,))):
    return lax.dot_general(a, b, (dims, ((), ())), preferred_element_type=F32)


NT = ((1,), (1,))
TN = ((0,), (0,))


def call(body, outs, operands, smem=(), flops=0, name=None, specs=None, out_specs=None, grid=1, limit=LIMIT):
    vmem = pl.BlockSpec(memory_space=pltpu.VMEM)
    sm = pl.BlockSpec(memory_space=pltpu.SMEM)
    nbytes = sum(a.size * a.dtype.itemsize for a in operands) + sum(
        o.size * o.dtype.itemsize for o in outs
    )
    return pl.pallas_call(
        body,
        out_shape=outs,
        grid=(grid,) if specs else (),
        in_specs=[sm] * len(smem) + (specs or [vmem] * len(operands)),
        out_specs=out_specs or [vmem] * len(outs),
        compiler_params=pltpu.CompilerParams(vmem_limit_bytes=limit << 20),
        cost_estimate=pl.CostEstimate(flops=flops, bytes_accessed=nbytes, transcendentals=0),
        name=name,
    )(*smem, *operands)


def shape(*dims, dtype=BF):
    return jax.ShapeDtypeStruct(dims, dtype)


def head(h):
    return slice(h * DH, (h + 1) * DH)


def position():
    return lax.broadcasted_iota(jnp.int32, (TOK, DH), 0)


def column(rate, offset, low_flag, high_flag):
    row = position()
    flag = jnp.where(row < TOK // 2, low_flag, high_flag)
    return jnp.where(flag > 0, jnp.exp(-rate * offset.astype(F32)), 0.0)


def intra_mask(same):
    t = lax.broadcasted_iota(jnp.int32, (TOK, TOK), 0)
    j = lax.broadcasted_iota(jnp.int32, (TOK, TOK), 1)
    distance = t - j
    half = TOK // 2
    crossing = jnp.logical_and(t >= half, j < half)
    allowed = jnp.logical_and(
        distance >= 0, jnp.logical_or(jnp.logical_not(crossing), same > 0)
    )
    return jnp.maximum(distance, 0).astype(F32), allowed


def where_am_i():
    span = lax.axis_index("seq")
    chip = lax.div(span, 2)
    return lax.rem(span, 2), lax.div(chip, 4), lax.rem(chip, 4)


def doc_flags(docs):
    span = lax.axis_index("seq")
    first, second = docs[2 * span], docs[2 * span + 1]
    prev = docs[jnp.maximum(2 * span - 1, 0)]
    coming = docs[jnp.minimum(2 * span + 2, 63)]
    tests = (first == second, first == prev, second == prev, first == coming, second == coming)
    return [jnp.where(t, 1, 0) for t in tests]


def lanes(h):
    return pl.ds(pl.multiple_of(h * DH, DH), DH)


def local_state_body(rates, docs, k, v, own, theirs):
    flags = doc_flags(docs)
    core, _, _ = where_am_i()
    for i in range(HEADS):
        h = lax.rem(core * 4 + i, HEADS)
        w = column(rates[h], TOK - 1 - position(), flags[0], 1)
        weighted = (k[:, lanes(h)].astype(F32) * w).astype(BF)
        state = dot(weighted, v[:, lanes(h)], TN)
        if i < 4:
            own[head(i), :] = state
        else:
            theirs[head(i - 4), :] = state.astype(BF)


def local_out_body(rates, docs, q, k, v, att, out):
    flags = doc_flags(docs)
    core, _, _ = where_am_i()
    distance, allowed = intra_mask(flags[0])
    for h in range(HEADS):
        intra = jnp.where(allowed, jnp.exp(-rates[h] * distance), 0.0)
        a = (dot(q[:, head(h)], k[:, head(h)], NT) * intra).astype(BF)
        att[h] = a
        out[:, head(h)] = dot(a, v[:, head(h)])


def pick(core, h, own, other):
    rows = slice((h % 4) * DH, (h % 4 + 1) * DH)
    mine = core == (h // 4)
    return jnp.where(mine, own[rows, :].astype(F32), other[rows, :].astype(F32)).astype(BF)


def forward_body(rates, docs, q, local, own, other, out, normed):
    flags = doc_flags(docs)
    core, _, _ = where_am_i()
    for h in range(HEADS):
        w = column(rates[h], position() + 1, flags[1], flags[2])
        o = local[:, head(h)] + w * dot(q[:, head(h)], pick(core, h, own, other))
        out[:, head(h)] = o
        inv = lax.rsqrt(jnp.mean(o * o, axis=-1, keepdims=True) + EPSILON)
        normed[:, head(h)] = (o * inv).astype(BF)


def grad_attn_body(rates, docs, q, out, part, part_other, grad, own, theirs):
    flags = doc_flags(docs)
    core, _, _ = where_am_i()
    for i in range(HEADS):
        h = lax.rem(core * 4 + i, HEADS)
        at = lanes(h)
        o = out[:, at]
        inv = lax.rsqrt(jnp.mean(o * o, axis=-1, keepdims=True) + EPSILON)
        normal = o * inv
        g = part[:, at] + part_other[:, at].astype(F32)
        inner = jnp.mean(g * normal, axis=-1, keepdims=True)
        ga = (inv * (g - normal * inner)).astype(BF)
        grad[:, at] = ga
        w = column(rates[h], position(), 1, flags[0])
        weighted = (q[:, at].astype(F32) * w).astype(BF)
        state = dot(weighted, ga, TN)
        if i < 4:
            own[head(i), :] = state
        else:
            theirs[head(i - 4), :] = state.astype(BF)


def grad_local_body(rates, docs, q, k, v, att, grad, own, other, dq, dk, dv):
    flags = doc_flags(docs)
    core, _, _ = where_am_i()
    distance, allowed = intra_mask(flags[0])
    for h in range(HEADS):
        intra = jnp.where(allowed, jnp.exp(-rates[h] * distance), 0.0)
        ga = grad[:, head(h)]
        ds = (dot(ga, v[:, head(h)], NT) * intra).astype(BF)
        w = column(rates[h], position() + 1, flags[1], flags[2])
        dq[:, head(h)] = (
            dot(ds, k[:, head(h)]) + w * dot(ga, pick(core, h, own, other), NT)
        ).astype(BF)
        dk[:, head(h)] = dot(ds, q[:, head(h)], TN)
        dv[:, head(h)] = dot(att[h], ga, TN)


def grad_rest_body(rates, docs, k, v, dkl, dvl, own, other, dk, dv):
    flags = doc_flags(docs)
    core, _, _ = where_am_i()
    for h in range(HEADS):
        w = column(rates[h], TOK - position(), flags[3], flags[4])
        back = pick(core, h, own, other)
        dk[:, head(h)] = (dkl[:, head(h)] + w * dot(v[:, head(h)], back, NT)).astype(BF)
        dv[:, head(h)] = (dvl[:, head(h)] + w * dot(k[:, head(h)], back)).astype(BF)


PAIR = 2 * ROWS
DEEP = CHIPS * ROWS


def split_body(g, eye, gm, gmt, gt):
    core, y, x = where_am_i()
    first, second = jnp.where(core == 0, x, y), jnp.where(core == 0, y, x)
    step, stride = jnp.where(core == 0, 1, 4), jnp.where(core == 0, 4, 1)

    def pair(p, first, second, step, stride, side):
        at = lax.rem(second + REL[p // 2], 4) * stride
        cols = []
        for k in (2 * (p % 2), 2 * (p % 2) + 1):
            chip = at + lax.rem(first + REL[k], 4) * step
            cols.append(g[:, pl.ds(pl.multiple_of(chip * PAIR, DH), PAIR)])
        low = jnp.concatenate([c[:, :ROWS] for c in cols], 1)
        high = jnp.concatenate([c[:, ROWS:] for c in cols], 1)
        return jnp.where(side == 0, low, high)

    for p in range(8):
        rows = slice(p * PAIR, (p + 1) * PAIR)
        block = pair(p, second, first, stride, step, 1 - core)
        gt[rows, :] = dot(eye[...], block, NT).astype(BF)
        for part in range(3):
            lane = 3 * p + part
            row = DEEP + (lane // 2) * TOK
            gt[row : row + TOK, (lane % 2) * DH : (lane % 2 + 1) * DH] = block[:, head(part)]
        block = pair(p, first, second, step, stride, core)
        gm[:, rows] = block
        gmt[rows, :] = dot(eye[...], block, NT).astype(BF)


def join_body(*refs):
    out, at = refs[-1], 0
    for ref in refs[:-1]:
        out[at : at + ref.shape[0], :] = ref[...]
        at += ref.shape[0]


def join(*arrays):
    rows = sum(a.shape[0] for a in arrays)
    return call(join_body, [shape(rows, arrays[0].shape[1])], arrays, name="join")[0]


def project_body(gm, gr, *refs):
    weights, other, own = refs[:8], refs[8], refs[9]
    w = jnp.concatenate([ref[...] for ref in weights], 0)
    chunks = [gr[c * TOK : (c + 1) * TOK, :] for c in range(DEEP // TOK)]
    both = dot(jnp.concatenate([jnp.concatenate(chunks, 1), gm[...]], 0), w)
    other[...] = both[:TOK].astype(BF)
    own[...] = both[TOK:]


def part_of(gm, gr, nm, nr):
    return dot(gm[...], nm[...]) + dot(gr[...], nr[...])


def scatter_two_body(gm0, gm1, gr0, gr1, nm, nr, a, b):
    a[...] = part_of(gm0, gr0, nm, nr).astype(BF)
    b[...] = part_of(gm1, gr1, nm, nr).astype(BF)


def scatter_near_body(gm0, gm1, gr0, gr1, nm, nr, from_minus, from_plus, plus, minus):
    plus[...] = (part_of(gm0, gr0, nm, nr) + from_minus[...].astype(F32)).astype(BF)
    minus[...] = (part_of(gm1, gr1, nm, nr) + from_plus[...].astype(F32)).astype(BF)


CUT = ROWS // 2


def scatter_own_body(gm0, gm1, gr0, gr1, nm, nr, low0, low1, high0, high1, *outs):
    mine, minus, plus, far0, far1 = outs
    v = part_of(gm1, gr1, nm, nr) + high0[...].astype(F32) + high1[...].astype(F32)
    plus[...] = v[:ROWS].astype(BF)
    far0[...] = v[ROWS : ROWS + CUT].astype(BF)
    far1[...] = v[ROWS + CUT :].astype(BF)
    v = part_of(gm0, gr0, nm, nr) + low0[...].astype(F32) + low1[...].astype(F32)
    mine[...] = v[:ROWS]
    minus[...] = v[ROWS:].astype(BF)


def last_near_body(plus, minus, from_minus, from_plus, plus_out, minus_out):
    plus_out[:CUT, :] = plus[:CUT, :] + from_minus[...]
    plus_out[CUT:, :] = plus[CUT:, :]
    minus_out[:CUT, :] = minus[:CUT, :]
    minus_out[CUT:, :] = minus[CUT:, :] + from_plus[...]


def last_sum_body(own, from_minus, from_plus, out):
    out[...] = (own[...] + from_minus[...].astype(F32) + from_plus[...].astype(F32)).astype(BF)


def part(body, p, q, outs, terms, more=(), name=None):
    gmt, gr, normed, normed_other = terms
    vmem = pl.BlockSpec(memory_space=pltpu.VMEM)
    blocks = [pl.BlockSpec((PAIR, TOK), lambda _, i=i: (i, 0)) for i in (p, q, p, q)]
    return call(
        body,
        outs,
        [gmt, gmt, gr, gr, normed, normed_other, *more],
        flops=16 * TOK * ROWS * FEAT,
        name=name,
        specs=blocks + [vmem] * (2 + len(more)),
    )


def scan_tools(rates, docs, backward):
    core, y, x = where_am_i()
    half = core * 4
    if backward:
        core, y, x = 1 - core, 3 - y, 3 - x

    def doc(s):
        s = jnp.clip(s, 0, 31)
        return docs[62 - 2 * s] if backward else docs[2 * s + 1]

    def weight(h, steps, one, two, valid=True):
        equal = jnp.logical_and(doc(one) == doc(two), valid)
        steps = jnp.maximum(steps, 0).astype(F32) * float(TOK)
        decay = jnp.exp(-(rates[half + h] * steps) * jnp.ones((1, DH), F32))
        return jnp.where(equal, decay, 0.0)

    return core, y, x, y * 4 + x, weight


def scan_total_body(backward):
    def body(rates, docs, own, got, total, low):
        core, y, x, chip, weight = scan_tools(rates, docs, backward)
        for h in range(4):
            w = weight(h, jnp.int32(1), 2 * chip, 2 * chip + 1)
            first = jnp.where(core == 0, w, 1.0)
            second = jnp.where(core == 0, 1.0, w)
            t = first * own[head(h), :] + second * got[head(h), :].astype(F32)
            total[head(h), :] = t
            low[head(h), :] = t.astype(BF)

    return body


def scan_row_body(backward):
    def body(rates, docs, total, near1, near2, near3, before, low):
        core, y, x, chip, weight = scan_tools(rates, docs, backward)
        row, last, entry = y * 4, y * 8 + 7, 2 * chip - 1
        for h in range(4):
            t = total[head(h), :]
            whole = weight(h, 2 * (3 - x), 2 * chip + 1, last) * t
            ahead = jnp.zeros_like(t)
            for n, near in ((1, near1), (2, near2), (3, near3)):
                at = lax.rem(x + 4 - n, 4)
                v = near[head(h), :].astype(F32)
                whole = whole + weight(h, 2 * (3 - at), 2 * (row + at) + 1, last) * v
                ahead = ahead + weight(h, 2 * (x - 1 - at), 2 * (row + at) + 1, entry, at < x) * v
            before[head(h), :] = ahead
            low[head(h), :] = whole.astype(BF)

    return body


def scan_end_body(backward):
    def body(rates, docs, before, own, got, up1, up2, mine, other):
        core, y, x, chip, weight = scan_tools(rates, docs, backward)
        entry = 2 * chip - 1
        for h in range(4):
            ahead = before[head(h), :]
            for n, up in ((1, up1), (2, up2)):
                at = y * 4 - 4 * n + 3
                w = weight(h, 2 * (chip - 1 - at), 2 * at + 1, entry, y >= n)
                ahead = ahead + w * up[head(h), :].astype(F32)
            first = jnp.where(core == 0, own[head(h), :], got[head(h), :].astype(F32))
            after = first + weight(h, jnp.int32(1), 2 * chip, entry, chip > 0) * ahead
            mine[head(h), :] = jnp.where(core == 0, ahead, after).astype(BF)
            other[head(h), :] = jnp.where(core == 0, after, ahead).astype(BF)

    return body


WIDE, NARROW = shape(HALF, DH, dtype=F32), shape(HALF, DH)


class Scan:
    def __init__(self, sm, backward):
        self.sm, self.backward = sm, backward
        self.sign = -1 if backward else 1
        self.name = "back" if backward else "fwd"

    def total(self, own, theirs):
        self.own, self.got = own, send(theirs, PARTNER)
        self.sum, low = call(
            scan_total_body(self.backward),
            [WIDE, NARROW],
            [self.own, self.got],
            self.sm,
            name=self.name + "_total",
        )
        return low

    def along_x(self, low):
        return [send(low, x_by(self.sign * n)) for n in (1, 2, 3)]

    def row(self, near):
        self.before, low = call(
            scan_row_body(self.backward),
            [WIDE, NARROW],
            [self.sum, *near],
            self.sm,
            name=self.name + "_row",
        )
        return low

    def along_y(self, low):
        return [send(low, y_by(self.sign * n)) for n in (1, 2)]

    def end(self, up):
        mine, other = call(
            scan_end_body(self.backward),
            [NARROW, NARROW],
            [self.before, self.own, self.got, *up],
            self.sm,
            name=self.name + "_end",
        )
        return mine, send(other, PARTNER)


def after(arrays):
    return lax.optimization_barrier(tuple(arrays))


def local(query_rows, key_rows, value_rows, grad_out, out_weight, decay_rates, doc_blocks):
    q, k, v, g = query_rows[0], key_rows[0], value_rows[0], grad_out[0]
    sm = (decay_rates, doc_blocks[0])
    unit = 2 * HEADS * TOK * DH * DH
    states = [WIDE, NARROW]
    rows = shape(TOK, FEAT)
    wide_rows = shape(TOK, FEAT, dtype=F32)
    pair = shape(PAIR, FEAT)
    small = shape(CUT, FEAT)

    minus, plus, far = (send(out_weight, first_by(n)) for n in (1, -1, 2))
    fwd = Scan(sm, False)
    state = call(
        local_state_body, states, [k, v], sm, flops=unit, name="state_local", limit=60
    )
    low = fwd.total(*state)

    low, g, minus, plus, far = after((low, g, minus, plus, far))
    own_low = join(out_weight, minus)
    near = fwd.along_x(low)
    minus_low, plus_low = send(own_low, second_by(1)), send(own_low, second_by(-1))
    gm, gmt, gt = call(
        split_body,
        [shape(TOK, DEEP), shape(DEEP, TOK), shape(2 * DEEP, TOK)],
        [g, jnp.eye(PAIR, dtype=BF)],
        flops=4 * PAIR * PAIR * TOK * 8,
        name="split",
    )
    own_high = join(plus, far)
    *near, gm, gt, own_high, minus_low, plus_low = after(
        (*near, gm, gt, own_high, minus_low, plus_low)
    )
    low = fwd.row(near)
    gr = send(gt, PARTNER)
    up = fwd.along_y(low)
    minus_high, plus_high = send(own_high, second_by(1)), send(own_high, second_by(-1))

    att, out_local = call(
        local_out_body,
        [shape(HEADS, TOK, TOK), wide_rows],
        [q, k, v],
        sm,
        flops=4 * unit,
        name="attend",
    )
    *up, own_high, att, out_local = after((*up, own_high, att, out_local))
    own, other = fwd.end(up)
    out, normed = call(
        forward_body,
        [wide_rows, rows],
        [q, out_local, own, other],
        sm,
        flops=unit,
        name="carry",
    )
    normed_other = send(normed, PARTNER)
    normed_other, minus_high, plus_high = after((normed_other, minus_high, plus_high))
    far_low, far_high = send(minus_low, second_by(1)), send(plus_high, second_by(-1))

    terms = [gmt, gr, normed, normed_other]
    low, high = part(scatter_two_body, 6, 7, [pair] * 2, terms, name="part_far")
    near_in = [send(low, second_by(1)), send(high, second_by(-1))]
    plus, minus = part(scatter_two_body, 5, 2, [pair] * 2, terms, name="part_free")
    gm, plus, minus = after((gm, plus, minus))
    weights = [own_low, own_high, minus_low, minus_high, plus_low, plus_high, far_low, far_high]
    free_in = [send(plus, second_by(1)), send(minus, second_by(-1))]
    vmem = pl.BlockSpec(memory_space=pltpu.VMEM)
    part_other, part_own = call(
        project_body,
        [rows, wide_rows],
        [gm, gr, *weights],
        flops=4 * TOK * DEEP * FEAT,
        name="project",
        grid=4,
        specs=[vmem, pl.BlockSpec((DEEP, TOK), lambda _: (1, 0))]
        + [pl.BlockSpec((PAIR, FEAT // 4), lambda n: (0, n))] * 8,
        out_specs=[pl.BlockSpec((TOK, FEAT // 4), lambda n: (0, n))] * 2,
    )
    *near_in, part_other, part_own = after((*near_in, part_other, part_own))
    plus, minus = part(scatter_near_body, 4, 3, [pair] * 2, terms, near_in, name="part_near")
    late_in = [send(plus, second_by(1)), send(minus, second_by(-1))]
    part_other = send(part_other, PARTNER)
    grad, *back = call(
        grad_attn_body,
        [rows, *states],
        [q, out, part_own, part_other],
        sm,
        flops=unit,
        name="grad_attn",
    )
    back_scan = Scan(sm, True)
    low = back_scan.total(*back)
    low, *free_in = after((low, *free_in))
    near = back_scan.along_x(low)
    dq, dkl, dvl = call(
        grad_local_body,
        [rows, wide_rows, wide_rows],
        [q, k, v, att, grad, own, other],
        sm,
        flops=9 * unit,
        name="grad_local",
    )
    *near, dq, dkl, dvl = after((*near, dq, dkl, dvl))
    low = back_scan.row(near)
    *terms, low = after((*terms, low))
    up = back_scan.along_y(low)

    mine, minus, plus, far0, far1 = part(
        scatter_own_body,
        0,
        1,
        [shape(ROWS, FEAT, dtype=F32)] + [shape(ROWS, FEAT)] * 2 + [small] * 2,
        terms,
        [late_in[0], free_in[1], free_in[0], late_in[1]],
        name="part_own",
    )
    far0, far1 = send(far0, first_by(1)), send(far1, first_by(-1))
    plus, minus = call(
        last_near_body, [shape(ROWS, FEAT)] * 2, [plus, minus, far0, far1], name="part_last"
    )
    plus, minus = send(plus, first_by(1)), send(minus, first_by(-1))
    (total,) = call(last_sum_body, [shape(ROWS, FEAT)], [mine, plus, minus], name="part_sum")
    scale = (2 * 32 * TOK) ** (-0.5)
    swapped = lax.ppermute(total, "dp", [(0, 1), (1, 0)])
    grad_weight = (total.astype(F32) + swapped.astype(F32)) * scale
    back_own, back_other = back_scan.end(up)
    dk, dv = call(
        grad_rest_body,
        [rows, rows],
        [k, v, dkl, dvl, back_own, back_other],
        sm,
        flops=2 * unit,
        name="grad_rest",
    )
    return dq[None], dk[None], dv[None], grad_weight


def solution(mesh):
    in_specs = (
        P("dp", "seq", "head"),
        P("dp", "seq", "head"),
        P("dp", "seq", "head"),
        P("dp", "seq", None),
        P("seq", "head"),
        P("head"),
        P("dp", None),
    )
    out_specs = (
        P("dp", "seq", "head"),
        P("dp", "seq", "head"),
        P("dp", "seq", "head"),
        P("seq", "head"),
    )
    return jax.shard_map(local, mesh=mesh, in_specs=in_specs, out_specs=out_specs, check_vma=False)
```
